32 devices in a mesh: layer: 2 (over x), expert: 4 (over y, core), col: 4 (over z).
Axes of the slice: x: 2, y: 2, z: 4, core: 2. Of those that a mesh axis runs over, the one named last changes fastest.
Arguments:
- target_weights: bfloat16 [8, 7168, 2048], P(('layer', 'expert'), None, 'col'), parts along dimension 0, may hold values from -36 to 36
- factors: float32 [8, 7168, 128], P(('layer', 'expert'), 'col'), parts along dimension 0, may hold values from -0.5 to 0.5
- bases: float32 [64, 128, 2048], P('layer', None, 'col'), parts along dimension 0, may hold values from -6 to 6
- coefficients: float32 [8, 32], P(('layer', 'expert')), parts along dimension 0, may hold values from -1 to 1
Outputs:
- new_factors: float32 [8, 7168, 128], P(('layer', 'expert'), 'col'), parts along dimension 0
- new_bases: float32 [64, 128, 2048], P('layer', None, 'col'), parts along dimension 0
- new_coefficients: float32 [8, 32], P(('layer', 'expert')), parts along dimension 0
- losses: float32 [4], P('layer'), parts along dimension 0
The draws below stay inside these ranges and needn't reach their ends.
There are 2 independent parts, one for each index of `layer`. The reference program is written for one: setup_inputs(seed, part) draws one part's arguments, and reference() takes and returns one part's arrays. A program takes and returns all parts, laid end to end along the dimension named above; each array names one. Nothing has to cross between parts.
All inputs are finite; a program needn't handle non-finite values.
Results may differ from the reference program's by a relative error of at most 0.0003.
Values sent between devices are 32-bit elements; how exact they have to be, the bound alone decides.
A program may use at most 128 MiB of HBM per device.

```python
import jax
import jax.numpy as jnp
from jax import lax

D = 7168
H = 2048
R = 128
K = 32
ITERS = 2
EXPERTS = 4


def draw_target_weights(key, part):
    keys = jax.random.split(key, 2)
    values = jnp.clip(jax.random.normal(keys[0], (EXPERTS, D, H), jnp.float32), -4.0, 4.0)
    expert_pos = jnp.arange(EXPERTS, dtype=jnp.float32) / (EXPERTS - 1)
    column_pos = jnp.arange(H, dtype=jnp.float32) / (H - 1)
    expert_scale = jnp.sqrt(1.0 + 2.0 * expert_pos)
    column_scale = jnp.sqrt(1.0 + 2.0 * column_pos) * jax.random.uniform(keys[1], (H,), jnp.float32, 0.7, 1.4)
    values = values * expert_scale[:, None, None] * column_scale[None, None, :]
    return values.astype(jnp.bfloat16)


def shard_levels(stream_key, shape, cuts, smallest, high):
    level = 1.0
    for dim, shards_of in cuts:
        heights = jax.random.uniform(jax.random.fold_in(jax.random.fold_in(stream_key, 6), dim), (shards_of,), jnp.float32, smallest / len(cuts), high / len(cuts))
        level = level * jnp.repeat(jnp.exp(heights), shape[dim] // shards_of).reshape((-1,) + (1,) * (len(shape) - 1 - dim))
    return level


def noise(key, dims, scale, reach, cuts=(), held_as=jnp.bfloat16):
    gain = shard_levels(key, dims, cuts, -0.22, 0.18) if cuts else 1.0
    result = jax.random.normal(key, dims, jnp.float32) * scale * gain
    return jnp.minimum(jnp.maximum(result, -reach), reach).astype(held_as)


def setup_inputs(seed: int = 0, part: int = 0) -> dict:
    key_list = jax.random.split(jax.random.key(seed), 5)
    part_keys = jax.random.split(jax.random.fold_in(key_list[4], part), 5)
    target_weights = draw_target_weights(jax.random.fold_in(jax.random.fold_in(key_list[4], part), 71), part)
    factors = noise(part_keys[1], (EXPERTS, D, R), R ** -0.5, 0.5, ((0, 4), (1, 4)), jnp.float32)
    bases = noise(part_keys[2], (K, R, H), 1.0, 6.0, ((2, 4),), jnp.float32)
    coefficients = noise(part_keys[3], (EXPERTS, K), K ** -0.5, 1.0, ((0, 4),), jnp.float32)
    return {"target_weights": target_weights, "factors": factors, "bases": bases, "coefficients": coefficients}


LEARN_RATE = 0.01
BETA_ONE = 0.9
BETA_TWO = 0.999
EPSILON = 0.0001
HIGHEST = lax.Precision.HIGHEST

def adam_update(parameter, gradient, moment_one, moment_two, iteration):
    moment_one = BETA_ONE * moment_one + (1.0 - BETA_ONE) * gradient
    moment_two = BETA_TWO * moment_two + (1.0 - BETA_TWO) * gradient * gradient
    first_hat = moment_one / (1.0 - BETA_ONE ** (iteration + 1))
    second_hat = moment_two / (1.0 - BETA_TWO ** (iteration + 1))
    parameter = parameter - LEARN_RATE * first_hat / (jnp.sqrt(second_hat) + EPSILON)
    return (parameter, moment_one, moment_two)

def expert_terms(operands):
    factor, mixed, target = operands
    residual = jnp.dot(factor, mixed, precision=HIGHEST) - target.astype(jnp.float32)
    loss_part = jnp.sum(residual * residual)
    gradient = residual / H
    d_factor = jnp.dot(gradient, mixed.T, precision=HIGHEST)
    d_mixed = jnp.dot(factor.T, gradient, precision=HIGHEST)
    return (loss_part, d_factor, d_mixed)

def reference(target_weights, factors, bases, coefficients):
    factor_one = jnp.zeros_like(factors)
    factor_two = jnp.zeros_like(factors)
    basis_one = jnp.zeros_like(bases)
    basis_two = jnp.zeros_like(bases)
    coef_one = jnp.zeros_like(coefficients)
    coef_two = jnp.zeros_like(coefficients)
    loss_list = []
    for iteration in range(ITERS):
        mixed = jnp.tanh(jnp.einsum('ek,krh->erh', coefficients, bases, precision=HIGHEST))
        loss_parts, d_factors, d_mixed = lax.map(expert_terms, (factors, mixed, target_weights))
        loss_list.append(jnp.sum(loss_parts) * (1.0 / (2.0 * EXPERTS * D * H)))
        d_pre = d_mixed * (1.0 - mixed * mixed)
        d_bases = jnp.einsum('ek,erh->krh', coefficients, d_pre, precision=HIGHEST)
        d_coef = jnp.einsum('krh,erh->ek', bases, d_pre, precision=HIGHEST)
        factors, factor_one, factor_two = adam_update(factors, d_factors, factor_one, factor_two, iteration)
        bases, basis_one, basis_two = adam_update(bases, d_bases, basis_one, basis_two, iteration)
        coefficients, coef_one, coef_two = adam_update(coefficients, d_coef, coef_one, coef_two, iteration)
    return (factors, bases, coefficients, jnp.stack(loss_list))
```

```python
import jax
import jax.numpy as jnp
from jax import lax
from jax.sharding import PartitionSpec as P

LEARN_RATE = 0.01
BETA_ONE = 0.9
BETA_TWO = 0.999
EPSILON = 0.0001
HIGHEST = lax.Precision.HIGHEST


def adam_first(parameter, g):
    return parameter - LEARN_RATE * g / (jnp.abs(g) + EPSILON)


def adam_second(parameter, g_one, g_two):
    first = (BETA_ONE * (1.0 - BETA_ONE) * g_one + (1.0 - BETA_ONE) * g_two) * (1.0 / (1.0 - BETA_ONE**2))
    second = (
        BETA_TWO * (1.0 - BETA_TWO) * g_one * g_one + (1.0 - BETA_TWO) * g_two * g_two
    ) * (1.0 / (1.0 - BETA_TWO**2))
    return parameter - LEARN_RATE * first / (jnp.sqrt(second) + EPSILON)


def pieces(x, count=3):
    out = []
    for _ in range(count):
        piece = lax.reduce_precision(x, 8, 7)
        out.append(piece.astype(jnp.bfloat16))
        x = x - piece
    return out


def left_dot(target, mixed):
    total = 0.0
    for piece in pieces(mixed):
        total = total + lax.dot_general(
            target, piece, (((1,), (1,)), ((), ())), preferred_element_type=jnp.float32
        )
    return total


def down_dot(full, target):
    r = full.shape[1]
    stacked = jnp.concatenate(pieces(full), axis=1)
    parts = lax.dot_general(
        stacked, target, (((0,), (0,)), ((), ())), preferred_element_type=jnp.float32
    )
    return parts[:r] + parts[r : 2 * r] + parts[2 * r :]


def outer_basis(coef_all, d_pre_all):
    total = coef_all[0][:, None, None] * d_pre_all[0][None]
    for e in range(1, coef_all.shape[0]):
        total = total + coef_all[e][:, None, None] * d_pre_all[e][None]
    return total


def shards(target_weights, factors, bases, coefficients):
    target = target_weights[0]
    own = factors[0]
    experts = lax.axis_size("expert")
    cols = lax.axis_size("col")
    me = lax.axis_index("expert")
    d, h = target.shape[0], target.shape[1] * cols
    k = bases.shape[0]
    scale = 1.0 / h

    coef_all = lax.all_gather(coefficients[0], "expert", axis=0)
    full = lax.all_gather(own, "col", axis=0, tiled=True)
    coef = coefficients[0]

    def mix(c, b):
        return jnp.tanh(jnp.sum(c[:, None, None] * b, axis=0))

    def own_gradient(mixed, rows):
        gram = jnp.dot(mixed, mixed.T, precision=HIGHEST)
        r = gram.shape[0]
        part = left_dot(target, mixed).reshape(cols, -1, r)
        joined = jnp.concatenate([part, jnp.broadcast_to(gram, (cols, r, r))], axis=1)
        summed = lax.psum_scatter(joined, "col", scatter_dimension=0, tiled=False)
        return (jnp.dot(rows, summed[-r:], precision=HIGHEST) - summed[:-r]) * scale

    def pre_gradient(mixed, whole):
        gram = lax.dot_general(whole, whole, (((0,), (0,)), ((), ())), precision=HIGHEST)
        d_mixed = jnp.dot(gram, mixed, precision=HIGHEST) - down_dot(whole, target)
        return d_mixed * scale * (1.0 - mixed * mixed)

    def loss_of(mixed, whole):
        residual = jnp.dot(whole, mixed, precision=HIGHEST) - target.astype(jnp.float32)
        return jnp.sum(residual * residual)

    mixed_one = mix(coef, bases)
    g_factor_one = own_gradient(mixed_one, own)
    d_pre_one = pre_gradient(mixed_one, full)
    d_pre_one_all = lax.all_gather(d_pre_one, "expert", axis=0)
    d_coef_one = jnp.sum(bases * d_pre_one[None], axis=(1, 2))
    g_coef_one = jnp.sum(lax.all_gather(d_coef_one, ("expert", "col"), axis=0).reshape(experts, cols, k), axis=1)
    bases_two = adam_first(bases, outer_basis(coef_all, d_pre_one_all))
    coef_all_two = adam_first(coef_all, g_coef_one)
    coef_two = lax.dynamic_index_in_dim(coef_all_two, me, 0, keepdims=False)
    own_two = adam_first(own, g_factor_one)
    full_two = lax.all_gather(own_two, "col", axis=0, tiled=True)
    loss_one = loss_of(mixed_one, full)

    mixed_two = mix(coef_two, bases_two)
    g_factor_two = own_gradient(mixed_two, own_two)
    d_pre_two = pre_gradient(mixed_two, full_two)
    d_pre_two_all = lax.all_gather(d_pre_two, "expert", axis=0)
    d_coef_two = jnp.sum(bases_two * d_pre_two[None], axis=(1, 2))
    loss_two = loss_of(mixed_two, full_two)
    message = jnp.concatenate([d_coef_two, jnp.stack([loss_one, loss_two])])
    gathered = lax.all_gather(message, ("expert", "col"), axis=0)
    g_coef_two = jnp.sum(gathered.reshape(experts, cols, k + 2), axis=1)
    losses = jnp.sum(g_coef_two[:, k:], axis=0) * (1.0 / (2.0 * experts * d * h))
    coef_all_three = adam_second(coef_all_two, g_coef_one, g_coef_two[:, :k])
    coef_three = lax.dynamic_slice_in_dim(coef_all_three, me, 1, 0)
    bases_three = adam_second(
        bases_two, outer_basis(coef_all, d_pre_one_all), outer_basis(coef_all_two, d_pre_two_all)
    )
    own_three = adam_second(own_two, g_factor_one, g_factor_two)
    return (own_three[None], bases_three, coef_three, losses)


def solution(mesh):
    return jax.shard_map(
        shards,
        mesh=mesh,
        in_specs=(
            P(("layer", "expert"), None, "col"),
            P(("layer", "expert"), "col", None),
            P("layer", None, "col"),
            P(("layer", "expert"), None),
        ),
        out_specs=(
            P(("layer", "expert"), "col", None),
            P("layer", None, "col"),
            P(("layer", "expert"), None),
            P("layer"),
        ),
        check_vma=False,
    )
```

```python
import functools

import jax
import jax.numpy as jnp
from jax import lax
from jax.experimental import pallas as pl
from jax.experimental.pallas import tpu as pltpu
from jax.sharding import PartitionSpec as P

LEARN_RATE = 0.01
BETA_ONE = 0.9
BETA_TWO = 0.999
EPSILON = 0.0001
HIGHEST = lax.Precision.HIGHEST
MESH = pl.DeviceIdType.MESH
F32 = jnp.float32
BF16 = jnp.bfloat16


def adam_first(parameter, g):
    return parameter - LEARN_RATE * g / (jnp.abs(g) + EPSILON)


def adam_second(parameter, g_one, g_two):
    first = (BETA_ONE * (1.0 - BETA_ONE) * g_one + (1.0 - BETA_ONE) * g_two) * (1.0 / (1.0 - BETA_ONE**2))
    second = (
        BETA_TWO * (1.0 - BETA_TWO) * g_one * g_one + (1.0 - BETA_TWO) * g_two * g_two
    ) * (1.0 / (1.0 - BETA_TWO**2))
    return parameter - LEARN_RATE * first / (jnp.sqrt(second) + EPSILON)


def pieces(x, count=3):
    out = []
    for _ in range(count):
        piece = x.astype(BF16)
        out.append(piece)
        x = x - piece.astype(F32)
    return out


def contract(a, b, dims):
    return lax.dot_general(a, b, (dims, ((), ())), preferred_element_type=F32)


def fold(x, r):
    return x[:, :r] + x[:, r : 2 * r] + x[:, 2 * r :]


def fold_rows(x, r):
    return x[:r] + x[r : 2 * r] + x[2 * r :]


def kernel(
    n, experts, t_hbm, f_hbm, b_hbm, c_in, f_out, b_out, c_out, l_out,
    target, bases, full, part, landed, d_pre, c_one, c_two, d_coef, loss_in, g_one, gram_sum,
    mixed, mixed_cut, loss_sum, load_sem, ag_send, ag_recv, rs_send, rs_recv, ex_send, ex_recv, co_send, co_recv,
):
    me = lax.axis_index("col")
    mine = lax.axis_index("expert")
    rows, r = f_out.shape
    d, hl = target.shape
    k_count = bases.shape[0]
    scale = 1.0 / (hl * n)
    table = experts * k_count

    loads = [
        pltpu.make_async_copy(f_hbm, full.at[0, pl.ds(pl.multiple_of(me * rows, 8), rows)], load_sem.at[0]),
        pltpu.make_async_copy(b_hbm, bases, load_sem.at[1]),
        pltpu.make_async_copy(t_hbm, target, load_sem.at[2]),
        pltpu.make_async_copy(c_in, c_one.at[mine], load_sem.at[3]),
    ]
    for load in loads:
        load.start()
    barrier = pltpu.get_barrier_semaphore()
    for off in range(1, n):
        pl.semaphore_signal(barrier, inc=1, device_id={"col": lax.rem(me + off, n)}, device_id_type=MESH)
    for off in range(1, experts):
        pl.semaphore_signal(barrier, inc=1, device_id={"expert": lax.rem(mine + off, experts)}, device_id_type=MESH)
    pl.semaphore_wait(barrier, n + experts - 2)

    def shard_copy(it, way, s, shard):
        place = full.at[it, pl.ds(pl.multiple_of(shard * rows, 8), rows)]
        return pltpu.make_async_remote_copy(
            src_ref=place, dst_ref=place, send_sem=ag_send.at[it, way, s], recv_sem=ag_recv.at[it, way, s],
            device_id={"col": me + 1 - 2 * way}, device_id_type=MESH,
        )

    def gather_step(it, t):
        for way in range(2):
            shard = me - t * (1 - 2 * way)
            after = me + 1 - 2 * way
            inside = (shard >= 0) & (shard < n)

            if t >= 1:
                @pl.when(inside)
                def _():
                    shard_copy(it, way, t - 1, shard).wait_recv()

            if t <= n - 2:
                @pl.when(inside & (after >= 0) & (after < n))
                def _():
                    shard_copy(it, way, t, shard).start()

    def gather_sent(it):
        for way in range(2):
            for s in range(n - 1):
                shard = me - s * (1 - 2 * way)
                after = me + 1 - 2 * way

                @pl.when((shard >= 0) & (shard < n) & (after >= 0) & (after < n))
                def _():
                    shard_copy(it, way, s, shard).wait_send()

    def part_copy(it, way, s, j):
        return pltpu.make_async_remote_copy(
            src_ref=part.at[j], dst_ref=landed.at[way, s], send_sem=rs_send.at[it, way, s],
            recv_sem=rs_recv.at[it, way, s], device_id={"col": me + 1 - 2 * way}, device_id_type=MESH,
        )

    def scatter_step(it, t):
        for way in range(2):
            place = me if way == 0 else n - 1 - me
            s = t - place
            j = n - 1 - s if way == 0 else s

            @pl.when((place > 0) & (s >= 0))
            def _():
                part_copy(it, way, s, j).wait_recv()
                part[j] = part[j] + landed[way, s]

            if t <= n - 2:
                @pl.when(s >= 0)
                def _():
                    part_copy(it, way, s, j).start()

    def scatter_sent(it):
        for way in range(2):
            place = me if way == 0 else n - 1 - me
            for t in range(n - 1):
                s = t - place

                @pl.when(s >= 0)
                def _():
                    part_copy(it, way, s, n - 1 - s if way == 0 else s).wait_send()

    def expert_copy(ref, kind, off):
        place = ref.at[mine]
        return pltpu.make_async_remote_copy(
            src_ref=place, dst_ref=place, send_sem=ex_send.at[kind, off - 1], recv_sem=ex_recv.at[kind, off - 1],
            device_id={"expert": lax.rem(mine + off, experts)}, device_id_type=MESH,
        )

    def expert_start(ref, kind):
        for off in range(1, experts):
            expert_copy(ref, kind, off).start()

    def expert_wait(ref, kind):
        for off in range(1, experts):
            expert_copy(ref, kind, off).wait()

    def coef_copy(it, off):
        place = d_coef.at[it, me]
        return pltpu.make_async_remote_copy(
            src_ref=place, dst_ref=place, send_sem=co_send.at[it, off - 1], recv_sem=co_recv.at[it, off - 1],
            device_id={"col": lax.rem(me + off, n)}, device_id_type=MESH,
        )

    def mix(c_ref, b_ref):
        for q in range(0, hl, 128):
            def add(k, total):
                return total + c_ref[mine, pl.ds(k, 1), :] * b_ref[k, :, q : q + 128]

            mixed[:, q : q + 128] = jnp.tanh(lax.fori_loop(0, k_count, add, jnp.zeros((r, 128), F32)))
        for i, piece in enumerate(pieces(mixed[...])):
            mixed_cut[i * r : (i + 1) * r, :] = piece

    step = rows // 4 if (rows // 4) % 16 == 0 else rows

    def project():
        cut = mixed_cut[...]
        gram = fold_rows(fold(contract(cut, cut, ((1,), (1,))), r), r)
        for j in range(n):
            part[j, rows : rows + r, :] = gram

        def block(i, carry):
            at = pl.ds(pl.multiple_of(i * step, 16), step)
            value = fold(contract(target[at, :], mixed_cut[...], ((1,), (1,))), r)
            j = i // (rows // step)
            part[j, pl.ds(pl.multiple_of((i - j * (rows // step)) * step, 8), step), :] = value
            return carry

        lax.fori_loop(0, d // step, block, 0)

    def absorb(it, shard):
        half = rows // 2

        def block(i, carry):
            at = pl.ds(pl.multiple_of(shard * rows + i * half, 16), half)
            cut = jnp.concatenate(pieces(full[it, at, :]), axis=1)
            gram_sum[...] += contract(cut, jnp.concatenate([target[at, :], cut], axis=1), ((0,), (0,)))
            return carry

        lax.fori_loop(0, 2, block, 0)

    def absorb_step(it, t):
        if t == 0:
            gram_sum[...] = jnp.zeros_like(gram_sum)
            absorb(it, me)
        else:
            for way in range(2):
                shard = me - t * (1 - 2 * way)

                @pl.when((shard >= 0) & (shard < n))
                def _():
                    absorb(it, shard)

    def pre_gradient(it):
        total = fold_rows(gram_sum[...], r)
        gram = fold(total[:, hl:], r)
        now = mixed[...]
        d_mixed = jnp.dot(gram, now, precision=HIGHEST, preferred_element_type=F32) - total[:, :hl]
        d_pre[it, mine] = d_mixed * scale * (1.0 - now * now)

    def loss_of(it):
        loss_sum[...] = jnp.zeros_like(loss_sum)

        def block(i, carry):
            at = pl.ds(pl.multiple_of(i * 256, 256), 256)
            one, two = pieces(full[it, at, :], 2)
            wide = jnp.concatenate([one, two, one, two], axis=1)
            tall = jnp.concatenate(
                [mixed_cut[:r], mixed_cut[:r], mixed_cut[r : 2 * r], mixed_cut[r : 2 * r]], axis=0
            )
            residual = contract(wide, tall, ((1,), (0,))) - target[at, :].astype(F32)
            loss_sum[...] += jnp.sum((residual * residual).reshape(32, 8, hl), axis=0)
            return carry

        lax.fori_loop(0, d // 256, block, 0)
        total = loss_sum[:, 0:128]
        for q in range(128, hl, 128):
            total = total + loss_sum[:, q : q + 128]
        loss_in[mine, it * 8 : it * 8 + 8, :] = total

    def combine(c_ref, it, k, q):
        total = c_ref[0, pl.ds(k, 1), :] * d_pre[it, 0, :, q : q + 128]
        for e in range(1, experts):
            total = total + c_ref[e, pl.ds(k, 1), :] * d_pre[it, e, :, q : q + 128]
        return total

    def coef_rows(it, k, q, values):
        for e in range(experts):
            row = jnp.sum(values * d_pre[it, e, :, q : q + 128], axis=0, keepdims=True)
            at = (it, me, pl.ds(e * k_count + k, 1), slice(None))
            if q == 0:
                d_coef[at] = row
            else:
                d_coef[at] = d_coef[at] + row

    def coef_sum(it):
        total = d_coef[it, 0]
        for c in range(1, n):
            total = total + d_coef[it, c]
        return jnp.broadcast_to(jnp.sum(total, axis=1, keepdims=True), total.shape)

    def factor_gradient(i):
        at = pl.ds(pl.multiple_of(i * step, 8), step)
        before = full[0, pl.ds(pl.multiple_of(me * rows + i * step, 8), step), :]
        return at, before

    loads[0].wait()
    gather_step(0, 0)
    loads[3].wait()
    expert_start(c_one, 0)
    loads[1].wait()
    mix(c_one, bases)
    loads[2].wait()
    project()
    scatter_step(0, 0)
    absorb_step(0, 0)
    for t in range(1, n):
        gather_step(0, t)
        if t < n - 1:
            scatter_step(0, t)
        absorb_step(0, t)
    pre_gradient(0)
    expert_wait(c_one, 0)
    expert_start(d_pre.at[0], 1)
    scatter_step(0, n - 1)

    def factor_one(i, carry):
        at, before = factor_gradient(i)
        gram = part[me, rows : rows + r, :]
        g = (jnp.dot(before, gram, precision=HIGHEST, preferred_element_type=F32) - part[me, at, :]) * scale
        g_one[at, :] = g
        full[1, pl.ds(pl.multiple_of(me * rows + i * step, 8), step), :] = adam_first(before, g)
        return carry

    lax.fori_loop(0, rows // step, factor_one, 0)
    gather_step(1, 0)
    loss_of(0)
    scatter_sent(0)
    gather_sent(0)
    expert_wait(d_pre.at[0], 1)

    def bases_one(k, carry):
        for q in range(0, hl, 128):
            values = bases[k, :, q : q + 128]
            b_out[k, :, q : q + 128] = adam_first(values, combine(c_one, 0, k, q))
            coef_rows(0, k, q, values)
        return carry

    lax.fori_loop(0, k_count, bases_one, 0)
    d_coef[0, me, table : table + 8, :] = jnp.zeros((8, 128), F32)
    for off in range(1, n):
        coef_copy(0, off).start()
    absorb_step(1, 0)
    for off in range(1, n):
        coef_copy(0, off).wait()
    c_two[...] = adam_first(c_one[...], coef_sum(0)[:table].reshape(experts, k_count, 128))
    mix(c_two, b_out)
    if n > 1:
        gather_step(1, 1)
    project()
    scatter_step(1, 0)
    absorb_step(1, 1)
    for t in range(2, n):
        gather_step(1, t)
        scatter_step(1, t - 1)
        absorb_step(1, t)
    pre_gradient(1)
    expert_start(d_pre.at[1], 2)
    loss_of(1)
    expert_start(loss_in, 3)
    expert_wait(d_pre.at[1], 2)
    expert_wait(loss_in, 3)

    def bases_two(k, carry):
        for q in range(0, hl, 128):
            values = b_out[k, :, q : q + 128]
            coef_rows(1, k, q, values)
            b_out[k, :, q : q + 128] = adam_second(values, combine(c_one, 0, k, q), combine(c_two, 1, k, q))
        return carry

    lax.fori_loop(0, k_count, bases_two, 0)
    losses = loss_in[0]
    for e in range(1, experts):
        losses = losses + loss_in[e]
    for it in range(2):
        d_coef[1, me, table + it : table + it + 1, :] = jnp.sum(losses[it * 8 : it * 8 + 8], axis=0, keepdims=True)
    d_coef[1, me, table + 2 : table + 8, :] = jnp.zeros((6, 128), F32)
    for off in range(1, n):
        coef_copy(1, off).start()
    scatter_step(1, n - 1)

    def factor_two(i, carry):
        at, _ = factor_gradient(i)
        before = full[1, pl.ds(pl.multiple_of(me * rows + i * step, 8), step), :]
        gram = part[me, rows : rows + r, :]
        g = (jnp.dot(before, gram, precision=HIGHEST, preferred_element_type=F32) - part[me, at, :]) * scale
        f_out[at, :] = adam_second(before, g_one[at, :], g)
        return carry

    lax.fori_loop(0, rows // step, factor_two, 0)
    for off in range(1, n):
        coef_copy(1, off).wait()
    total = coef_sum(1)
    l_out[...] = total[table : table + 8]
    first = coef_sum(0)[:table].reshape(experts, k_count, 128)
    c_two[...] = adam_second(c_two[...], first, total[:table].reshape(experts, k_count, 128))
    c_out[...] = c_two[mine]
    scatter_sent(1)
    gather_sent(1)


def shards(target_weights, factors, bases, coefficients):
    n, experts = lax.axis_size("col"), lax.axis_size("expert")
    _, d, hl = target_weights.shape
    _, rows, r = factors.shape
    k = bases.shape[0]
    anywhere = pl.BlockSpec(memory_space=pl.ANY)
    local = pl.BlockSpec(memory_space=pltpu.VMEM)
    dma = pltpu.SemaphoreType.DMA
    new_factors, new_bases, new_coef, losses = pl.pallas_call(
        functools.partial(kernel, n, experts),
        out_shape=(
            jax.ShapeDtypeStruct((rows, r), F32),
            jax.ShapeDtypeStruct(bases.shape, F32),
            jax.ShapeDtypeStruct((k, 128), F32),
            jax.ShapeDtypeStruct((8, 128), F32),
        ),
        in_specs=[anywhere, anywhere, anywhere, anywhere],
        out_specs=(local, local, local, local),
        scratch_shapes=[
            pltpu.VMEM((d, hl), BF16),
            pltpu.VMEM(bases.shape, F32),
            pltpu.VMEM((2, d, r), F32),
            pltpu.VMEM((n, rows + r, r), F32),
            pltpu.VMEM((2, n - 1, rows + r, r), F32),
            pltpu.VMEM((2, experts, r, hl), F32),
            pltpu.VMEM((experts, k, 128), F32),
            pltpu.VMEM((experts, k, 128), F32),
            pltpu.VMEM((2, n, experts * k + 8, 128), F32),
            pltpu.VMEM((experts, 16, 128), F32),
            pltpu.VMEM((rows, r), F32),
            pltpu.VMEM((3 * r, hl + 3 * r), F32),
            pltpu.VMEM((r, hl), F32),
            pltpu.VMEM((3 * r, hl), BF16),
            pltpu.VMEM((8, hl), F32),
            dma((4,)),
            dma((2, 2, n - 1)),
            dma((2, 2, n - 1)),
            dma((2, 2, n - 1)),
            dma((2, 2, n - 1)),
            dma((4, experts - 1)),
            dma((4, experts - 1)),
            dma((2, n - 1)),
            dma((2, n - 1)),
        ],
        compiler_params=pltpu.CompilerParams(
            collective_id=0, has_side_effects=True, vmem_limit_bytes=66000000
        ),
    )(target_weights[0], factors[0], bases, jnp.broadcast_to(coefficients[0][:, None], (k, 128)))
    total = losses[:2, 0]
    return (new_factors[None], new_bases, new_coef[:, 0][None], total * (1.0 / (2.0 * experts * d * hl * n)))


def solution(mesh):
    return jax.shard_map(
        shards,
        mesh=mesh,
        in_specs=(
            P(("layer", "expert"), None, "col"),
            P(("layer", "expert"), "col", None),
            P("layer", None, "col"),
            P(("layer", "expert"), None),
        ),
        out_specs=(
            P(("layer", "expert"), "col", None),
            P("layer", None, "col"),
            P(("layer", "expert"), None),
            P("layer"),
        ),
        check_vma=False,
    )
```

```python
import functools

import jax
import jax.numpy as jnp
from jax import lax
from jax.experimental import pallas as pl
from jax.experimental.pallas import tpu as pltpu
from jax.sharding import PartitionSpec as P

LEARN_RATE = 0.01
BETA_ONE = 0.9
BETA_TWO = 0.999
EPSILON = 0.0001
HIGHEST = lax.Precision.HIGHEST
MESH = pl.DeviceIdType.MESH
F32 = jnp.float32
BF16 = jnp.bfloat16


def adam_first(parameter, g):
    return parameter - LEARN_RATE * g / (jnp.abs(g) + EPSILON)


def adam_second(parameter, g_one, g_two):
    first = (BETA_ONE * (1.0 - BETA_ONE) * g_one + (1.0 - BETA_ONE) * g_two) * (1.0 / (1.0 - BETA_ONE**2))
    second = (
        BETA_TWO * (1.0 - BETA_TWO) * g_one * g_one + (1.0 - BETA_TWO) * g_two * g_two
    ) * (1.0 / (1.0 - BETA_TWO**2))
    return parameter - LEARN_RATE * first / (jnp.sqrt(second) + EPSILON)


def pieces(x, count=3):
    out = []
    for _ in range(count):
        piece = x.astype(BF16)
        out.append(piece)
        x = x - piece.astype(F32)
    return out


def contract(a, b, dims):
    return lax.dot_general(a, b, (dims, ((), ())), preferred_element_type=F32)


def fold(x, r):
    return x[:, :r] + x[:, r : 2 * r] + x[:, 2 * r :]


def fold_rows(x, r):
    return x[:r] + x[r : 2 * r] + x[2 * r :]


def kernel(
    n, experts, t_hbm, f_hbm, b_hbm, c_in, f_out, b_out, c_out, l_out,
    target, bases, full, part, landed, d_pre, c_one, c_two, d_coef, loss_in, g_one, gram_sum,
    mixed, mixed_cut, loss_sum, load_sem, ag_send, ag_recv, rs_send, rs_recv, ex_send, ex_recv, co_send, co_recv,
):
    me = lax.axis_index("col")
    mine = lax.axis_index("expert")
    rows, r = f_out.shape
    d, hl = target.shape
    k_count = bases.shape[0]
    scale = 1.0 / (hl * n)
    table = experts * k_count

    loads = [
        pltpu.make_async_copy(f_hbm, full.at[0, pl.ds(pl.multiple_of(me * rows, 8), rows)], load_sem.at[0]),
        pltpu.make_async_copy(b_hbm, bases, load_sem.at[1]),
        pltpu.make_async_copy(t_hbm, target, load_sem.at[2]),
        pltpu.make_async_copy(c_in, c_one.at[mine], load_sem.at[3]),
    ]
    for load in loads:
        load.start()
    barrier = pltpu.get_barrier_semaphore()
    for off in range(1, n):
        pl.semaphore_signal(barrier, inc=1, device_id={"col": lax.rem(me + off, n)}, device_id_type=MESH)
    for off in range(1, experts):
        pl.semaphore_signal(barrier, inc=1, device_id={"expert": lax.rem(mine + off, experts)}, device_id_type=MESH)
    pl.semaphore_wait(barrier, n + experts - 2)

    def shard_copy(it, way, s, shard):
        place = full.at[it, pl.ds(pl.multiple_of(shard * rows, 8), rows)]
        return pltpu.make_async_remote_copy(
            src_ref=place, dst_ref=place, send_sem=ag_send.at[it, way, s], recv_sem=ag_recv.at[it, way, s],
            device_id={"col": me + 1 - 2 * way}, device_id_type=MESH,
        )

    def gather_step(it, t):
        for way in range(2):
            shard = me - t * (1 - 2 * way)
            after = me + 1 - 2 * way
            inside = (shard >= 0) & (shard < n)

            if t >= 1:
                @pl.when(inside)
                def _():
                    shard_copy(it, way, t - 1, shard).wait_recv()

            if t <= n - 2:
                @pl.when(inside & (after >= 0) & (after < n))
                def _():
                    shard_copy(it, way, t, shard).start()

    def gather_sent(it):
        for way in range(2):
            for s in range(n - 1):
                shard = me - s * (1 - 2 * way)
                after = me + 1 - 2 * way

                @pl.when((shard >= 0) & (shard < n) & (after >= 0) & (after < n))
                def _():
                    shard_copy(it, way, s, shard).wait_send()

    def part_copy(it, way, s, j):
        return pltpu.make_async_remote_copy(
            src_ref=part.at[j], dst_ref=landed.at[way, s], send_sem=rs_send.at[it, way, s],
            recv_sem=rs_recv.at[it, way, s], device_id={"col": me + 1 - 2 * way}, device_id_type=MESH,
        )

    def scatter_step(it, t):
        for way in range(2):
            place = me if way == 0 else n - 1 - me
            s = t - place
            j = n - 1 - s if way == 0 else s

            @pl.when((place > 0) & (s >= 0))
            def _():
                part_copy(it, way, s, j).wait_recv()
                part[j] = part[j] + landed[way, s]

            if t <= n - 2:
                @pl.when(s >= 0)
                def _():
                    part_copy(it, way, s, j).start()

    def scatter_sent(it):
        for way in range(2):
            place = me if way == 0 else n - 1 - me
            for t in range(n - 1):
                s = t - place

                @pl.when(s >= 0)
                def _():
                    part_copy(it, way, s, n - 1 - s if way == 0 else s).wait_send()

    def expert_copy(ref, kind, off):
        place = ref.at[mine]
        return pltpu.make_async_remote_copy(
            src_ref=place, dst_ref=place, send_sem=ex_send.at[kind, off - 1], recv_sem=ex_recv.at[kind, off - 1],
            device_id={"expert": lax.rem(mine + off, experts)}, device_id_type=MESH,
        )

    def expert_start(ref, kind):
        for off in range(1, experts):
            expert_copy(ref, kind, off).start()

    def expert_wait(ref, kind):
        for off in range(1, experts):
            expert_copy(ref, kind, off).wait()

    def coef_copy(it, off):
        place = d_coef.at[it, me]
        return pltpu.make_async_remote_copy(
            src_ref=place, dst_ref=place, send_sem=co_send.at[it, off - 1], recv_sem=co_recv.at[it, off - 1],
            device_id={"col": lax.rem(me + off, n)}, device_id_type=MESH,
        )

    def mix(it, c_ref, b_ref):
        for q in range(0, hl, 128):
            def add(k, total):
                return total + c_ref[mine, pl.ds(k, 1), :] * b_ref[k, :, q : q + 128]

            mixed[:, q : q + 128] = jnp.tanh(lax.fori_loop(0, k_count, add, jnp.zeros((r, 128), F32)))
        for i, piece in enumerate(pieces(mixed[...])):
            mixed_cut[it, i * r : (i + 1) * r, :] = piece

    step = rows // 4 if (rows // 4) % 16 == 0 else rows

    def project(it):
        cut = mixed_cut[it]
        gram = fold_rows(fold(contract(cut, cut, ((1,), (1,))), r), r)
        for j in range(n):
            part[j, rows : rows + r, :] = gram

        def block(i, carry):
            at = pl.ds(pl.multiple_of(i * step, 16), step)
            value = fold(contract(target[at, :], mixed_cut[it], ((1,), (1,))), r)
            j = i // (rows // step)
            part[j, pl.ds(pl.multiple_of((i - j * (rows // step)) * step, 8), step), :] = value
            return carry

        lax.fori_loop(0, d // step, block, 0)

    def absorb(it, shard):
        half = rows // 2

        def block(i, carry):
            at = pl.ds(pl.multiple_of(shard * rows + i * half, 16), half)
            cut = jnp.concatenate(pieces(full[it, at, :]), axis=1)
            gram_sum[...] += contract(cut, jnp.concatenate([target[at, :], cut], axis=1), ((0,), (0,)))
            return carry

        lax.fori_loop(0, 2, block, 0)

    def absorb_step(it, t):
        if t == 0:
            gram_sum[...] = jnp.zeros_like(gram_sum)
            absorb(it, me)
        else:
            for way in range(2):
                shard = me - t * (1 - 2 * way)

                @pl.when((shard >= 0) & (shard < n))
                def _():
                    absorb(it, shard)

    def pre_gradient(it):
        total = fold_rows(gram_sum[...], r)
        gram = fold(total[:, hl:], r)
        now = mixed[...]
        d_mixed = jnp.dot(gram, now, precision=HIGHEST, preferred_element_type=F32) - total[:, :hl]
        d_pre[it, mine] = d_mixed * scale * (1.0 - now * now)

    def loss_add(it, shard):
        def block(i, carry):
            at = pl.ds(pl.multiple_of(shard * rows + i * step, 16), step)
            one, two = pieces(full[it, at, :], 2)
            wide = jnp.concatenate([one, two, one, two], axis=1)
            upper, lower = mixed_cut[it, :r], mixed_cut[it, r : 2 * r]
            tall = jnp.concatenate([upper, upper, lower, lower], axis=0)
            residual = contract(wide, tall, ((1,), (0,))) - target[at, :].astype(F32)
            loss_sum[...] += jnp.sum((residual * residual).reshape(step // 8, 8, hl), axis=0)
            return carry

        lax.fori_loop(0, rows // step, block, 0)

    def loss_step(it, t):
        for way in range(2):
            shard = me - t * (1 - 2 * way)

            @pl.when((shard >= 0) & (shard < n))
            def _():
                loss_add(it, shard)

    def loss_close(it):
        total = loss_sum[:, 0:128]
        for q in range(128, hl, 128):
            total = total + loss_sum[:, q : q + 128]
        loss_in[mine, it * 8 : it * 8 + 8, :] = total
        loss_sum[...] = jnp.zeros_like(loss_sum)

    def combine(c_ref, it, k, q):
        total = c_ref[0, pl.ds(k, 1), :] * d_pre[it, 0, :, q : q + 128]
        for e in range(1, experts):
            total = total + c_ref[e, pl.ds(k, 1), :] * d_pre[it, e, :, q : q + 128]
        return total

    def coef_rows(it, k, q, values):
        for e in range(experts):
            row = jnp.sum(values * d_pre[it, e, :, q : q + 128], axis=0, keepdims=True)
            at = (it, me, pl.ds(e * k_count + k, 1), slice(None))
            if q == 0:
                d_coef[at] = row
            else:
                d_coef[at] = d_coef[at] + row

    def coef_sum(it):
        total = d_coef[it, 0]
        for c in range(1, n):
            total = total + d_coef[it, c]
        return jnp.broadcast_to(jnp.sum(total, axis=1, keepdims=True), total.shape)

    def factor_gradient(i):
        at = pl.ds(pl.multiple_of(i * step, 8), step)
        before = full[0, pl.ds(pl.multiple_of(me * rows + i * step, 8), step), :]
        return at, before

    loads[0].wait()
    gather_step(0, 0)
    loads[3].wait()
    expert_start(c_one, 0)
    loads[1].wait()
    mix(0, c_one, bases)
    loads[2].wait()
    project(0)
    scatter_step(0, 0)
    absorb_step(0, 0)
    for t in range(1, n):
        gather_step(0, t)
        if t < n - 1:
            scatter_step(0, t)
        absorb_step(0, t)
    pre_gradient(0)
    expert_wait(c_one, 0)
    expert_start(d_pre.at[0], 1)
    scatter_step(0, n - 1)

    def factor_one(i, carry):
        at, before = factor_gradient(i)
        gram = part[me, rows : rows + r, :]
        g = (jnp.dot(before, gram, precision=HIGHEST, preferred_element_type=F32) - part[me, at, :]) * scale
        g_one[at, :] = g
        full[1, pl.ds(pl.multiple_of(me * rows + i * step, 8), step), :] = adam_first(before, g)
        return carry

    lax.fori_loop(0, rows // step, factor_one, 0)
    gather_step(1, 0)
    scatter_sent(0)
    gather_sent(0)
    expert_wait(d_pre.at[0], 1)

    def bases_one(k, carry):
        for q in range(0, hl, 128):
            values = bases[k, :, q : q + 128]
            b_out[k, :, q : q + 128] = adam_first(values, combine(c_one, 0, k, q))
            coef_rows(0, k, q, values)
        return carry

    lax.fori_loop(0, k_count, bases_one, 0)
    d_coef[0, me, table : table + 8, :] = jnp.zeros((8, 128), F32)
    for off in range(1, n):
        coef_copy(0, off).start()
    gather_step(1, 1)
    absorb_step(1, 0)
    for off in range(1, n):
        coef_copy(0, off).wait()
    c_two[...] = adam_first(c_one[...], coef_sum(0)[:table].reshape(experts, k_count, 128))
    mix(1, c_two, b_out)
    project(1)
    scatter_step(1, 0)
    absorb_step(1, 1)
    loss_sum[...] = jnp.zeros_like(loss_sum)

    def loss_first(j, carry):
        loss_add(0, j)
        return carry

    for t in range(2, n):
        gather_step(1, t)
        if t < n - 1:
            scatter_step(1, t - 1)
            absorb_step(1, t)
            if t == 2:
                lax.fori_loop(0, n, loss_first, 0)
                loss_close(0)
                loss_add(1, me)
                loss_step(1, 1)
            loss_step(1, t)
    absorb_step(1, n - 1)
    pre_gradient(1)
    expert_start(d_pre.at[1], 2)
    scatter_step(1, n - 2)
    loss_step(1, n - 1)
    loss_close(1)
    expert_start(loss_in, 3)
    expert_wait(d_pre.at[1], 2)
    expert_wait(loss_in, 3)

    def coefs_two(k, carry):
        for q in range(0, hl, 128):
            coef_rows(1, k, q, b_out[k, :, q : q + 128])
        return carry

    lax.fori_loop(0, k_count, coefs_two, 0)
    losses = loss_in[0]
    for e in range(1, experts):
        losses = losses + loss_in[e]
    for it in range(2):
        d_coef[1, me, table + it : table + it + 1, :] = jnp.sum(losses[it * 8 : it * 8 + 8], axis=0, keepdims=True)
    d_coef[1, me, table + 2 : table + 8, :] = jnp.zeros((6, 128), F32)
    for off in range(1, n):
        coef_copy(1, off).start()

    def bases_two(k, carry):
        for q in range(0, hl, 128):
            values = b_out[k, :, q : q + 128]
            b_out[k, :, q : q + 128] = adam_second(values, combine(c_one, 0, k, q), combine(c_two, 1, k, q))
        return carry

    lax.fori_loop(0, k_count, bases_two, 0)
    scatter_step(1, n - 1)

    def factor_two(i, carry):
        at, _ = factor_gradient(i)
        before = full[1, pl.ds(pl.multiple_of(me * rows + i * step, 8), step), :]
        gram = part[me, rows : rows + r, :]
        g = (jnp.dot(before, gram, precision=HIGHEST, preferred_element_type=F32) - part[me, at, :]) * scale
        f_out[at, :] = adam_second(before, g_one[at, :], g)
        return carry

    lax.fori_loop(0, rows // step, factor_two, 0)
    for off in range(1, n):
        coef_copy(1, off).wait()
    total = coef_sum(1)
    l_out[...] = total[table : table + 8]
    first = coef_sum(0)[:table].reshape(experts, k_count, 128)
    c_two[...] = adam_second(c_two[...], first, total[:table].reshape(experts, k_count, 128))
    c_out[...] = c_two[mine]
    scatter_sent(1)
    gather_sent(1)


def shards(target_weights, factors, bases, coefficients):
    n, experts = lax.axis_size("col"), lax.axis_size("expert")
    _, d, hl = target_weights.shape
    _, rows, r = factors.shape
    k = bases.shape[0]
    anywhere = pl.BlockSpec(memory_space=pl.ANY)
    local = pl.BlockSpec(memory_space=pltpu.VMEM)
    dma = pltpu.SemaphoreType.DMA
    new_factors, new_bases, new_coef, losses = pl.pallas_call(
        functools.partial(kernel, n, experts),
        out_shape=(
            jax.ShapeDtypeStruct((rows, r), F32),
            jax.ShapeDtypeStruct(bases.shape, F32),
            jax.ShapeDtypeStruct((k, 128), F32),
            jax.ShapeDtypeStruct((8, 128), F32),
        ),
        in_specs=[anywhere, anywhere, anywhere, anywhere],
        out_specs=(local, local, local, local),
        scratch_shapes=[
            pltpu.VMEM((d, hl), BF16),
            pltpu.VMEM(bases.shape, F32),
            pltpu.VMEM((2, d, r), F32),
            pltpu.VMEM((n, rows + r, r), F32),
            pltpu.VMEM((2, n - 1, rows + r, r), F32),
            pltpu.VMEM((2, experts, r, hl), F32),
            pltpu.VMEM((experts, k, 128), F32),
            pltpu.VMEM((experts, k, 128), F32),
            pltpu.VMEM((2, n, experts * k + 8, 128), F32),
            pltpu.VMEM((experts, 16, 128), F32),
            pltpu.VMEM((rows, r), F32),
            pltpu.VMEM((3 * r, hl + 3 * r), F32),
            pltpu.VMEM((r, hl), F32),
            pltpu.VMEM((2, 3 * r, hl), BF16),
            pltpu.VMEM((8, hl), F32),
            dma((4,)),
            dma((2, 2, n - 1)),
            dma((2, 2, n - 1)),
            dma((2, 2, n - 1)),
            dma((2, 2, n - 1)),
            dma((4, experts - 1)),
            dma((4, experts - 1)),
            dma((2, n - 1)),
            dma((2, n - 1)),
        ],
        compiler_params=pltpu.CompilerParams(
            collective_id=0, has_side_effects=True, vmem_limit_bytes=66000000
        ),
    )(target_weights[0], factors[0], bases, jnp.broadcast_to(coefficients[0][:, None], (k, 128)))
    total = losses[:2, 0]
    return (new_factors[None], new_bases, new_coef[:, 0][None], total * (1.0 / (2.0 * experts * d * hl * n)))


def solution(mesh):
    return jax.shard_map(
        shards,
        mesh=mesh,
        in_specs=(
            P(("layer", "expert"), None, "col"),
            P(("layer", "expert"), "col", None),
            P("layer", None, "col"),
            P(("layer", "expert"), None),
        ),
        out_specs=(
            P(("layer", "expert"), "col", None),
            P("layer", None, "col"),
            P(("layer", "expert"), None),
            P("layer"),
        ),
        check_vma=False,
    )
```
